128 devices in a mesh: band: 4 (over x_hi, core), feed: 32 (over y, z, x_lo).
Axes of the slice: x: 4 (x_hi: 2, x_lo: 2; x = x_hi * 2 + x_lo), y: 4, z: 4, core: 2. Of those that a mesh axis runs over, the one named last changes fastest.
Arguments:
- voltages: float32 [768, 2048, 128], P('band', 'feed'), may hold values from -6 to 6
- feed_cells: int32 [4096], replicated, may hold values from 0 to 4095, each once
- delays: int32 [768, 256], P('band'), may hold values from 0 to 63
Outputs:
- dedispersed: float32 [256, 1024, 64], P('band', 'feed')
The draws below stay inside these ranges and needn't reach their ends.
Inputs may be any that keep to these rules, and one draw needn't show every extreme that they name: `feed_cells`: a permutation of the cells of the 64 x 64 feed grid, so no two feeds share a cell.
All inputs are finite; a program needn't handle non-finite values.
Results may differ from the reference program's by a relative error of at most 0.0003.
Values sent between devices are 32-bit elements; how exact they have to be, the bound alone decides.
A program may use at most 128 MiB of HBM per device.

```python
import math
import jax
import jax.numpy as jnp
from jax import lax

FEEDS = 2048
CHANNELS = 768
FRAMES = 64
SIDE = 32
BEAMS = 1024
TRIALS = 256
GRID = 64


def with_ends(result, rng, smallest, high):
    index_at = [jax.random.randint(jax.random.fold_in(rng, axis), (), 0, length) for axis, length in enumerate(result.shape)]
    widest = result.shape.index(max(result.shape))
    neighbour = index_at[:widest] + [(index_at[widest] + 1) % result.shape[widest]] + index_at[widest + 1:]
    return result.at[tuple(index_at)].set(smallest).at[tuple(neighbour)].set(high)


def steps_of(key, shape, split, least, largest):
    factor_of = 1.0
    for position, parts in split:
        steps = jax.random.uniform(jax.random.fold_in(jax.random.fold_in(key, 6), position), (parts,), jnp.float32, least / len(split), largest / len(split))
        factor_of = factor_of * jnp.repeat(jnp.exp(steps), shape[position] // parts).reshape((-1,) + (1,) * (len(shape) - 1 - position))
    return factor_of


def scatter_about(rng, shape, spread, limit, split=(), kind=jnp.bfloat16):
    factor_of = steps_of(rng, shape, split, -0.22, 0.18) if split else 1.0
    entries = jax.random.normal(rng, shape, jnp.float32) * spread * factor_of
    return jnp.minimum(jnp.maximum(entries, -limit), limit).astype(kind)


def setup_inputs(seed: int = 0) -> dict:
    key_list = jax.random.split(jax.random.key(seed), 4)
    voltages = scatter_about(key_list[0], (CHANNELS, FEEDS, 2 * FRAMES), 1.0, 6.0, ((0, 4), (1, 32)), jnp.float32)
    feed_cells = jax.random.permutation(key_list[1], GRID * GRID).astype(jnp.int32)
    delays = with_ends(jax.random.randint(key_list[2], (CHANNELS, TRIALS), 0, FRAMES), jax.random.fold_in(key_list[2], 1), 0, FRAMES - 1).astype(jnp.int32)
    return dict(voltages=voltages, feed_cells=feed_cells, delays=delays)


def feed_offsets(feed_cells):
    cell_index = feed_cells[:FEEDS]
    cell_row = cell_index // GRID
    cell_col = cell_index % GRID
    beam_ids = jnp.arange(BEAMS, dtype=jnp.int32)
    beam_row = beam_ids // SIDE - SIDE // 2
    beam_col = beam_ids % SIDE - SIDE // 2
    return beam_row[:, None] * cell_row[None, :] + beam_col[:, None] * cell_col[None, :]

def steering(offsets, channel):
    residue = jnp.mod(offsets * (CHANNELS + channel), GRID * CHANNELS)
    phases = residue.astype(jnp.float32) * (2.0 * math.pi / (GRID * CHANNELS))
    factor = 1.0 / math.sqrt(FEEDS)
    return (jnp.cos(phases) * factor, jnp.sin(phases) * factor)

def reference(voltages, feed_cells, delays):
    highest = lax.Precision.HIGHEST
    offsets = feed_offsets(feed_cells)

    def beam_power(item):
        channel, voltage = item
        cosine, sine_part = steering(offsets, channel)
        with_cos = jnp.dot(cosine, voltage, precision=highest)
        with_sin = jnp.dot(sine_part, voltage, precision=highest)
        real_part = with_cos[:, :FRAMES] + with_sin[:, FRAMES:]
        imag_part = with_cos[:, FRAMES:] - with_sin[:, :FRAMES]
        return real_part * real_part + imag_part * imag_part
    powers = lax.map(beam_power, (jnp.arange(CHANNELS, dtype=jnp.int32), voltages))
    centred = powers - lax.optimization_barrier(jnp.mean(powers, axis=2, keepdims=True))
    frame_ids = jnp.arange(FRAMES, dtype=jnp.int32)
    wave = jnp.mod(frame_ids[:, None] * frame_ids[None, :], FRAMES).astype(jnp.float32) * (2.0 * math.pi / FRAMES)
    forward = jnp.concatenate([jnp.cos(wave), -jnp.sin(wave)], axis=1)
    spectra = jnp.dot(centred.reshape(CHANNELS * BEAMS, FRAMES), forward, precision=highest)
    spectra = spectra.reshape(CHANNELS, BEAMS, 2 * FRAMES)

    def one_bin(bin_index):
        residue = jnp.mod(delays * bin_index, FRAMES)
        phases = residue.astype(jnp.float32) * (2.0 * math.pi / FRAMES)
        shift_cos = jnp.cos(phases).T
        shift_sin = jnp.sin(phases).T
        spec_real = lax.dynamic_index_in_dim(spectra, bin_index, 2, False)
        spec_imag = lax.dynamic_index_in_dim(spectra, bin_index + FRAMES, 2, False)
        out_real = jnp.dot(shift_cos, spec_real, precision=highest) - jnp.dot(shift_sin, spec_imag, precision=highest)
        out_imag = jnp.dot(shift_cos, spec_imag, precision=highest) + jnp.dot(shift_sin, spec_real, precision=highest)
        return (out_real, out_imag)
    bins_real, bins_imag = lax.map(one_bin, frame_ids)
    series = jnp.einsum('kdb,kt->dbt', bins_real, jnp.cos(wave), precision=highest)
    series = series - jnp.einsum('kdb,kt->dbt', bins_imag, jnp.sin(wave), precision=highest)
    return series * (0.5 / (FRAMES * math.sqrt(CHANNELS)))
```

```python
import functools, math
import jax, jax.numpy as jnp, numpy as np
from jax import lax
from jax.experimental import pallas as pl
from jax.experimental.pallas import tpu as pltpu
from jax.sharding import PartitionSpec as P

FEEDS, CHANNELS, FRAMES, SIDE, BEAMS, GRID = 2048, 768, 64, 32, 1024, 64
F32, BF16 = jnp.float32, jnp.bfloat16


def halves(x):
    high = x.astype(BF16)
    return high, (x - high.astype(F32)).astype(BF16)


def steering_tables(channels):
    side = jnp.arange(SIDE, dtype=jnp.int32) - SIDE // 2
    cell = jnp.arange(GRID, dtype=jnp.int32)
    product = side[None, :, None] * cell[None, None, :] * (CHANNELS + channels)[:, None, None]
    phases = jnp.mod(product, GRID * CHANNELS).astype(F32) * (2.0 * math.pi / (GRID * CHANNELS))
    return jnp.concatenate([jnp.cos(phases), jnp.sin(phases)], axis=1)


def stacked(x):
    high, low = halves(x)
    return jnp.concatenate([high, low, high], axis=0)


def lane_sign(rows):
    lane = lax.broadcasted_iota(jnp.int32, (rows, 128), 1)
    return jnp.where(lane < FRAMES, 1.0, -1.0).astype(F32), lane < FRAMES


def beams_of(products, sign):
    return products[:SIDE] + pltpu.roll(products[SIDE:], FRAMES, 1) * sign


def beam_kernel(cells_ref, table_ref, volt_ref, out_ref, grid_ref, mid_ref):
    @pl.when(pl.program_id(0) == 0)
    def _():
        grid_ref[...] = jnp.zeros_like(grid_ref)

    def place(group, carry):
        for k in range(16):
            feed = group * 16 + k
            grid_ref[pl.ds(cells_ref[feed], 1), :] = volt_ref[group // 4, 0, pl.ds((group % 4) * 16 + k, 1), :]
        return carry

    lax.fori_loop(0, FEEDS // 16, place, 0)
    table_high, table_low = halves(table_ref[0])
    table = jnp.concatenate([table_high, table_high, table_low], axis=1)
    sign, low_lanes = lane_sign(SIDE)

    def over_columns(step, carry):
        pieces = []
        for k in range(2):
            row = step * 2 + k
            pieces.append(stacked(grid_ref[pl.ds(row * GRID, GRID), :]))
        products = jnp.dot(table, jnp.concatenate(pieces, axis=1), preferred_element_type=F32)
        for k in range(2):
            row = step * 2 + k
            mid_ref[pl.ds(row * SIDE, SIDE), :] = beams_of(products[:, k * 128 : (k + 1) * 128], sign)
        return carry

    lax.fori_loop(0, GRID // 2, over_columns, 0, unroll=4)
    for pair in range(SIDE // 2):
        pieces = [stacked(mid_ref[pl.ds(pair * 2 + k, GRID, stride=SIDE), :]) for k in range(2)]
        products = jnp.dot(table, jnp.concatenate(pieces, axis=1), preferred_element_type=F32)
        powers = []
        for k in range(2):
            beam = beams_of(products[:, k * 128 : (k + 1) * 128], sign)
            square = beam * beam
            powers.append(square + pltpu.roll(square, FRAMES, 1))
        out_ref[:, 0, pair, :] = jnp.where(low_lanes, powers[0], powers[1])


def beam_powers(feed_cells, tables, by_source):
    sources, chans = by_source.shape[:2]
    return pl.pallas_call(
        beam_kernel,
        out_shape=jax.ShapeDtypeStruct((SIDE, chans, SIDE // 2, 128), F32),
        grid_spec=pltpu.PrefetchScalarGridSpec(
            num_scalar_prefetch=1,
            grid=(chans,),
            in_specs=[
                pl.BlockSpec((1, 64, 64), lambda c, cells: (c, 0, 0)),
                pl.BlockSpec((sources, 1, 64, 128), lambda c, cells: (0, c, 0, 0)),
            ],
            out_specs=pl.BlockSpec((SIDE, 1, SIDE // 2, 128), lambda c, cells: (0, c, 0, 0)),
            scratch_shapes=[pltpu.VMEM((GRID * GRID, 128), F32), pltpu.VMEM((GRID * SIDE, 128), F32)],
        ),
        name="beam_powers",
    )(feed_cells, tables, by_source)


def dft_tables():
    t = np.arange(FRAMES)
    k = np.arange(1, 33)
    ang = 2.0 * np.pi * ((k[:, None] * t[None, :]) % FRAMES) / FRAMES
    fwd = np.concatenate([np.cos(ang), -np.sin(ang)], axis=0)
    weight = np.where(k == 32, 1.0, 2.0)[:, None]
    scale = 0.5 / (FRAMES * math.sqrt(CHANNELS)) / FEEDS
    inv = np.concatenate([np.cos(ang) * weight, -np.sin(ang) * weight], axis=0) * scale
    def pair(m):
        z = np.zeros_like(m)
        return np.block([[m, z], [z, m]]).astype(np.float32)
    return pair(fwd), pair(inv)


def split_const(m):
    high = m.astype(jnp.bfloat16)
    low = (m - high.astype(np.float32)).astype(jnp.bfloat16)
    return high, low


def shift_kernel(fwd_ref, inv_ref, delay_ref, pow_ref, out_ref, spec_ref, fold_ref, base_ref, turn_ref):
    nt = (((1,), (1,)), ((), ()))
    chans = pow_ref.shape[0]
    for pair in range(SIDE // 2):
        high, low = halves(pow_ref[:, pair, :])
        both = lax.dot_general(fwd_ref[...], high, nt, preferred_element_type=F32)
        spec = both[:128] + both[128:] + lax.dot_general(fwd_ref[:128], low, nt, preferred_element_type=F32)
        for odd in range(2):
            for part in range(2):
                rows = spec[(odd * 2 + part) * 32 : (odd * 2 + part + 1) * 32]
                at = pl.ds(part * 32 + pair * 2 + odd, 32, stride=64)
                spec_ref[0, at, :] = rows[:, :128]
                spec_ref[1, at, pl.ds(0, chans - 128)] = rows[:, 128:]
    angle = delay_ref[...].astype(F32) * (2.0 * math.pi / FRAMES)
    base_ref[0] = jnp.cos(angle)
    base_ref[1] = jnp.sin(angle)
    turn_ref[0] = base_ref[0]
    turn_ref[1] = base_ref[1]

    def one_bin(step, carry):
        at = pl.ds(pl.multiple_of(step * 64, 64), 64)
        spec = jnp.concatenate([spec_ref[0, at, :], spec_ref[1, at, pl.ds(0, chans - 128)]], axis=1)
        turned = jnp.concatenate([-spec[32:], spec[:32]], axis=0)
        total = None
        for value, part in ((spec, 0), (turned, 1)):
            high, low = halves(value)
            turn_high, turn_low = halves(turn_ref[part])
            both = jnp.dot(jnp.concatenate([high, low], axis=0), turn_high, preferred_element_type=F32)
            term = both[:64] + both[64:] + jnp.dot(high, turn_low, preferred_element_type=F32)
            total = term if total is None else total + term
        fold_ref[0, at, :] = total[:, :128]
        fold_ref[1, at, :] = total[:, 128:]
        real, imag = turn_ref[0], turn_ref[1]
        turn_ref[0] = real * base_ref[0] - imag * base_ref[1]
        turn_ref[1] = real * base_ref[1] + imag * base_ref[0]
        return carry

    lax.fori_loop(0, 32, one_bin, 0)
    for pair in range(SIDE // 2):
        for half in range(2):
            rows = [
                fold_ref[half, pl.ds(part * 32 + pair * 2 + odd, 32, stride=64), :]
                for odd in range(2) for part in range(2)
            ]
            high, low = halves(jnp.concatenate(rows, axis=0).T)
            series = (
                jnp.dot(high, inv_ref[:128], preferred_element_type=F32)
                + jnp.dot(high, inv_ref[128:], preferred_element_type=F32)
                + jnp.dot(low, inv_ref[:128], preferred_element_type=F32)
            )
            out_ref[pl.ds(half * 128, 128), pair, :] = series


def shifted_sums(powers, delays):
    fwd, inv = dft_tables()
    fwd = jnp.asarray(np.concatenate(split_const(fwd), axis=0))
    inv = jnp.asarray(np.concatenate(split_const(inv), axis=0))
    vmem = pl.BlockSpec(memory_space=pltpu.VMEM)
    chans, trials = delays.shape
    return pl.pallas_call(
        shift_kernel,
        out_shape=jax.ShapeDtypeStruct((trials, SIDE // 2, 128), F32),
        in_specs=[vmem] * 4,
        out_specs=vmem,
        scratch_shapes=[
            pltpu.VMEM((2, 2048, 128), F32),
            pltpu.VMEM((2, 2048, 128), F32),
            pltpu.VMEM((2, chans, trials), F32),
            pltpu.VMEM((2, chans, trials), F32),
        ],
        name="shifted_sums",
    )(fwd, inv, delays, powers)


def sum_kernel(in_ref, out_ref):
    for pair in range(SIDE // 2):
        total = in_ref[0, :, pair, :] + in_ref[1, :, pair, :] + in_ref[2, :, pair, :] + in_ref[3, :, pair, :]
        out_ref[:, 2 * pair, :] = total[:, :FRAMES]
        out_ref[:, 2 * pair + 1, :] = total[:, FRAMES:]


def summed(pieces):
    vmem = pl.BlockSpec(memory_space=pltpu.VMEM)
    return pl.pallas_call(
        sum_kernel,
        out_shape=jax.ShapeDtypeStruct((pieces.shape[1], SIDE, FRAMES), F32),
        in_specs=[vmem],
        out_specs=vmem,
        name="summed",
    )(pieces)


PIECES = 3


def body(voltages, feed_cells, delays):
    band_chans = voltages.shape[0]
    peers = lax.axis_size("feed")
    local_chans = band_chans // peers
    first = lax.axis_index("band") * band_chans + lax.axis_index("feed") * local_chans
    tables = steering_tables(first + jnp.arange(local_chans, dtype=jnp.int32))
    blocks = voltages.reshape(peers, local_chans, *voltages.shape[1:])
    span = local_chans // PIECES
    powers = []
    for piece in range(PIECES):
        at = slice(piece * span, (piece + 1) * span)
        moved = lax.all_to_all(blocks[:, at], "feed", 0, 0, tiled=True)
        powers.append(beam_powers(feed_cells, tables[at], moved))
    by_beam = lax.all_to_all(jnp.concatenate(powers, axis=1), "feed", 0, 0, tiled=True)
    partial = shifted_sums(by_beam.reshape(band_chans, SIDE // 2, 128), delays)
    owners = lax.axis_size("band")
    pieces = lax.all_to_all(partial.reshape(owners, -1, SIDE // 2, 128), "band", 0, 0, tiled=True)
    return summed(pieces)


def solution(mesh):
    placed = (P("band", "feed", None), P(), P("band", None))
    return jax.shard_map(
        body, mesh=mesh, in_specs=placed, out_specs=P("band", "feed", None), check_vma=False
    )
```

```python
import functools, math
import jax, jax.numpy as jnp, numpy as np
from jax import lax
from jax.experimental import pallas as pl
from jax.experimental.pallas import tpu as pltpu
from jax.sharding import PartitionSpec as P

FEEDS, CHANNELS, FRAMES, SIDE, BEAMS, GRID = 2048, 768, 64, 32, 1024, 64
F32, BF16 = jnp.float32, jnp.bfloat16


def halves(x):
    high = x.astype(BF16)
    return high, (x - high.astype(F32)).astype(BF16)


def steering_tables(channels):
    side = jnp.arange(SIDE, dtype=jnp.int32) - SIDE // 2
    cell = jnp.arange(GRID, dtype=jnp.int32)
    product = side[None, :, None] * cell[None, None, :] * (CHANNELS + channels)[:, None, None]
    phases = jnp.mod(product, GRID * CHANNELS).astype(F32) * (2.0 * math.pi / (GRID * CHANNELS))
    return jnp.concatenate([jnp.cos(phases), jnp.sin(phases)], axis=1)


def stacked(x):
    high, low = halves(x)
    return jnp.concatenate([high, low, high], axis=0)


def lane_sign(rows):
    lane = lax.broadcasted_iota(jnp.int32, (rows, 128), 1)
    return jnp.where(lane < FRAMES, 1.0, -1.0).astype(F32), lane < FRAMES


def beams_of(products, sign):
    return products[:SIDE] + pltpu.roll(products[SIDE:], FRAMES, 1) * sign


def dft_tables():
    t = np.arange(FRAMES)
    k = np.arange(1, 33)
    ang = 2.0 * np.pi * ((k[:, None] * t[None, :]) % FRAMES) / FRAMES
    fwd = np.concatenate([np.cos(ang), -np.sin(ang)], axis=0)
    weight = np.where(k == 32, 1.0, 2.0)[:, None]
    scale = 0.5 / (FRAMES * math.sqrt(CHANNELS)) / FEEDS
    inv = np.concatenate([np.cos(ang) * weight, -np.sin(ang) * weight], axis=0) * scale
    def pair(m):
        z = np.zeros_like(m)
        return np.block([[m, z], [z, m]]).astype(np.float32)
    return pair(fwd), pair(inv)


def split_const(m):
    high = m.astype(jnp.bfloat16)
    low = (m - high.astype(np.float32)).astype(jnp.bfloat16)
    return high, low


def shift_kernel(fwd_ref, inv_ref, delay_ref, pow_ref, out_ref, spec_ref, fold_ref, base_ref, turn_ref):
    nt = (((1,), (1,)), ((), ()))
    chans = pow_ref.shape[0]
    for pair in range(SIDE // 2):
        high, low = halves(pow_ref[:, pair, :])
        both = lax.dot_general(fwd_ref[...], high, nt, preferred_element_type=F32)
        spec = both[:128] + both[128:] + lax.dot_general(fwd_ref[:128], low, nt, preferred_element_type=F32)
        for odd in range(2):
            for part in range(2):
                rows = spec[(odd * 2 + part) * 32 : (odd * 2 + part + 1) * 32]
                at = pl.ds(part * 32 + pair * 2 + odd, 32, stride=64)
                spec_ref[0, at, :] = rows[:, :128]
                spec_ref[1, at, pl.ds(0, chans - 128)] = rows[:, 128:]
    angle = delay_ref[...].astype(F32) * (2.0 * math.pi / FRAMES)
    base_ref[0] = jnp.cos(angle)
    base_ref[1] = jnp.sin(angle)
    turn_ref[0] = base_ref[0]
    turn_ref[1] = base_ref[1]

    def one_bin(step, carry):
        at = pl.ds(pl.multiple_of(step * 64, 64), 64)
        spec = jnp.concatenate([spec_ref[0, at, :], spec_ref[1, at, pl.ds(0, chans - 128)]], axis=1)
        turned = jnp.concatenate([-spec[32:], spec[:32]], axis=0)
        total = None
        for value, part in ((spec, 0), (turned, 1)):
            high, low = halves(value)
            turn_high, turn_low = halves(turn_ref[part])
            both = jnp.dot(jnp.concatenate([high, low], axis=0), turn_high, preferred_element_type=F32)
            term = both[:64] + both[64:] + jnp.dot(high, turn_low, preferred_element_type=F32)
            total = term if total is None else total + term
        fold_ref[0, at, :] = total[:, :128]
        fold_ref[1, at, :] = total[:, 128:]
        real, imag = turn_ref[0], turn_ref[1]
        turn_ref[0] = real * base_ref[0] - imag * base_ref[1]
        turn_ref[1] = real * base_ref[1] + imag * base_ref[0]
        return carry

    lax.fori_loop(0, 32, one_bin, 0)
    for pair in range(SIDE // 2):
        for half in range(2):
            rows = [
                fold_ref[half, pl.ds(part * 32 + pair * 2 + odd, 32, stride=64), :]
                for odd in range(2) for part in range(2)
            ]
            high, low = halves(jnp.concatenate(rows, axis=0).T)
            series = (
                jnp.dot(high, inv_ref[:128], preferred_element_type=F32)
                + jnp.dot(high, inv_ref[128:], preferred_element_type=F32)
                + jnp.dot(low, inv_ref[:128], preferred_element_type=F32)
            )
            out_ref[pl.ds(half * 128, 128), pair, :] = series


def shifted_sums(powers, delays):
    fwd, inv = dft_tables()
    fwd = jnp.asarray(np.concatenate(split_const(fwd), axis=0))
    inv = jnp.asarray(np.concatenate(split_const(inv), axis=0))
    vmem = pl.BlockSpec(memory_space=pltpu.VMEM)
    chans, trials = delays.shape
    return pl.pallas_call(
        shift_kernel,
        out_shape=jax.ShapeDtypeStruct((trials, SIDE // 2, 128), F32),
        in_specs=[vmem] * 4,
        out_specs=vmem,
        scratch_shapes=[
            pltpu.VMEM((2, 2048, 128), F32),
            pltpu.VMEM((2, 2048, 128), F32),
            pltpu.VMEM((2, chans, trials), F32),
            pltpu.VMEM((2, chans, trials), F32),
        ],
        name="shifted_sums",
    )(fwd, inv, delays, powers)


def sum_kernel(in_ref, out_ref):
    for pair in range(SIDE // 2):
        total = in_ref[0, :, pair, :] + in_ref[1, :, pair, :] + in_ref[2, :, pair, :] + in_ref[3, :, pair, :]
        out_ref[:, 2 * pair, :] = total[:, :FRAMES]
        out_ref[:, 2 * pair + 1, :] = total[:, FRAMES:]


def summed(pieces):
    vmem = pl.BlockSpec(memory_space=pltpu.VMEM)
    return pl.pallas_call(
        sum_kernel,
        out_shape=jax.ShapeDtypeStruct((pieces.shape[1], SIDE, FRAMES), F32),
        in_specs=[vmem],
        out_specs=vmem,
        name="summed",
    )(pieces)


MESH = pl.DeviceIdType.MESH


def feed_of_cell(feed_cells):
    cells = feed_cells[:FEEDS]
    line = jnp.arange(GRID, dtype=jnp.int32)[:, None]
    rows = (cells[None, :] // GRID == line).astype(F32)
    cols = jnp.where(cells[None, :] % GRID == line, jnp.arange(1, FEEDS + 1, dtype=jnp.int32)[None, :], 0).astype(F32)
    found = lax.dot_general(rows, cols, (((1,), (1,)), ((), ())), precision=lax.Precision.HIGHEST)
    found = jnp.round(found).astype(jnp.int32).reshape(GRID * GRID)
    return jnp.where(found == 0, FEEDS, found - 1)


def peer_at(me, step):
    y, z, x = me // 8, (me // 2) % 4, me % 2
    return ((y + step // 8) % 4) * 8 + ((z + (step // 2) % 4) % 4) * 2 + (x + step % 2) % 2


def await_bytes(ref, sem):
    pltpu.make_async_copy(ref, ref, sem).wait()


def beams_of_grid(table, grid_ref, mid_ref, store):
    sign, low_lanes = lane_sign(SIDE)

    def over_columns(step, carry):
        pieces = []
        for k in range(2):
            pieces.append(stacked(grid_ref[pl.ds(pl.multiple_of((step * 2 + k) * GRID, GRID), GRID), :]))
        products = jnp.dot(table, jnp.concatenate(pieces, axis=1), preferred_element_type=F32)
        for k in range(2):
            at = pl.multiple_of((step * 2 + k) * SIDE, SIDE)
            mid_ref[pl.ds(at, SIDE), :] = beams_of(products[:, k * 128 : (k + 1) * 128], sign)
        return carry

    lax.fori_loop(0, GRID // 2, over_columns, 0, unroll=4)
    for pair in range(SIDE // 2):
        pieces = [stacked(mid_ref[pl.ds(pair * 2 + k, GRID, stride=SIDE), :]) for k in range(2)]
        products = jnp.dot(table, jnp.concatenate(pieces, axis=1), preferred_element_type=F32)
        powers = []
        for k in range(2):
            beam = beams_of(products[:, k * 128 : (k + 1) * 128], sign)
            square = beam * beam
            powers.append(square + pltpu.roll(square, FRAMES, 1))
        store(pair, jnp.where(low_lanes, powers[0], powers[1]))


def gather_kernel(peers, chans, source_ref, table_ref, volt_ref, out_ref, *scratch):
    land = scratch[:chans]
    powers = scratch[chans : 2 * chans]
    grid_ref, mid_ref, held, send_sem, land_sem, own_sem, pow_send, pow_land, out_sem = scratch[2 * chans :]
    me = lax.axis_index("feed")
    shard = FEEDS // peers
    barrier = pltpu.get_barrier_semaphore()

    def greet(step, carry):
        pl.semaphore_signal(barrier, inc=1, device_id={"feed": peer_at(me, step)}, device_id_type=MESH)
        return carry

    lax.fori_loop(1, peers, greet, 0)
    pl.semaphore_wait(barrier, peers - 1)
    mine = pl.ds(pl.multiple_of(me * shard, shard), shard)
    for c in range(chans):
        def send(step, carry, c=c):
            peer = peer_at(me, step)
            pltpu.make_async_remote_copy(
                src_ref=volt_ref.at[peer, c], dst_ref=land[c].at[mine], send_sem=send_sem.at[c],
                recv_sem=land_sem.at[c], device_id={"feed": peer}, device_id_type=MESH,
            ).start()
            return carry

        lax.fori_loop(1, peers, send, 0)
        pltpu.make_async_copy(volt_ref.at[me, c], land[c].at[mine], own_sem.at[c]).start()
        land[c][pl.ds(FEEDS, 8), :] = jnp.zeros((8, 128), F32)
    arriving = pl.ds(0, FEEDS - shard)
    for c in range(chans):
        await_bytes(land[c].at[arriving], land_sem.at[c])
        pltpu.make_async_copy(volt_ref.at[me, c], land[c].at[mine], own_sem.at[c]).wait()

        def place(group, carry, c=c):
            for k in range(16):
                cell = group * 16 + k
                grid_ref[pl.ds(cell, 1), :] = land[c][pl.ds(source_ref[cell], 1), :]
            return carry

        lax.fori_loop(0, GRID * GRID // 16, place, 0)
        table_high, table_low = halves(table_ref[c])

        def store(pair, power, c=c):
            powers[c][:, pair, :] = power

        beams_of_grid(jnp.concatenate([table_high, table_high, table_low], axis=1), grid_ref, mid_ref, store)
        row = me * chans + c

        def spread(step, carry, c=c):
            peer = peer_at(me, step)
            pltpu.make_async_remote_copy(
                src_ref=powers[c].at[peer], dst_ref=held.at[me * chans + c], send_sem=pow_send.at[c],
                recv_sem=pow_land, device_id={"feed": peer}, device_id_type=MESH,
            ).start()
            return carry

        lax.fori_loop(1, peers, spread, 0)
        held[row] = powers[c][me]
    await_bytes(held.at[pl.ds(0, (peers - 1) * chans)], pow_land)
    copy = pltpu.make_async_copy(held, out_ref, out_sem)
    copy.start()
    for c in range(chans):
        await_bytes(land[c].at[arriving], send_sem.at[c])
        await_bytes(powers[c].at[pl.ds(0, peers - 1)], pow_send.at[c])
    copy.wait()


def gathered_powers(source, tables, blocks):
    peers, chans, shard, lanes = blocks.shape
    kernel = functools.partial(gather_kernel, peers, chans)
    return pl.pallas_call(
        kernel,
        out_shape=jax.ShapeDtypeStruct((peers * chans, SIDE // 2, 128), F32),
        in_specs=[
            pl.BlockSpec(memory_space=pltpu.SMEM),
            pl.BlockSpec(memory_space=pltpu.VMEM),
            pl.BlockSpec(memory_space=pl.ANY),
        ],
        out_specs=pl.BlockSpec(memory_space=pl.ANY),
        scratch_shapes=[pltpu.VMEM((FEEDS + 8, 128), F32)] * chans
        + [pltpu.VMEM((SIDE, SIDE // 2, 128), F32)] * chans
        + [
            pltpu.VMEM((GRID * GRID, 128), F32),
            pltpu.VMEM((GRID * SIDE, 128), F32),
            pltpu.VMEM((peers * chans, SIDE // 2, 128), F32),
            pltpu.SemaphoreType.DMA((chans,)),
            pltpu.SemaphoreType.DMA((chans,)),
            pltpu.SemaphoreType.DMA((chans,)),
            pltpu.SemaphoreType.DMA((chans,)),
            pltpu.SemaphoreType.DMA,
            pltpu.SemaphoreType.DMA,
        ],
        compiler_params=pltpu.CompilerParams(collective_id=0, has_side_effects=True),
        name="gathered_powers",
    )(source, tables, blocks)


def body(voltages, feed_cells, delays):
    band_chans = voltages.shape[0]
    peers = lax.axis_size("feed")
    local_chans = band_chans // peers
    first = lax.axis_index("band") * band_chans + lax.axis_index("feed") * local_chans
    tables = steering_tables(first + jnp.arange(local_chans, dtype=jnp.int32))
    blocks = voltages.reshape(peers, local_chans, *voltages.shape[1:])
    by_beam = gathered_powers(feed_of_cell(feed_cells), tables, blocks)
    partial = shifted_sums(by_beam, delays)
    owners = lax.axis_size("band")
    pieces = lax.all_to_all(partial.reshape(owners, -1, SIDE // 2, 128), "band", 0, 0, tiled=True)
    return summed(pieces)


def solution(mesh):
    placed = (P("band", "feed", None), P(), P("band", None))
    return jax.shard_map(
        body, mesh=mesh, in_specs=placed, out_specs=P("band", "feed", None), check_vma=False
    )
```
